256 devices in a mesh: freq: 64 (over y, z, x_hi), inp: 4 (over x_lo, core).
Axes of the slice: x: 4 (x_hi: 2, x_lo: 2; x = x_hi * 2 + x_lo), y: 4, z: 8, core: 2. Of those that a mesh axis runs over, the one named last changes fastest.
Arguments:
- voltages: int32 [192, 2048, 1024], P('freq', None, 'inp'), may hold values from -128 to 127
- taps: float32 [12, 2048], replicated, may hold values from -0.013671875 to 0.013671875
- start: int32 [8, 2, 1024], replicated, may hold values from -127 to 127
Outputs:
- cleaned: bfloat16 [1024, 192, 2, 1024], P('freq', None, None, 'inp')
- ritz_matrix: float32 [1024, 8, 8], P('freq')
The draws below stay inside these ranges and needn't reach their ends.
Inputs may be any that keep to these rules, and one draw needn't show every extreme that they name: `voltages`: 8-bit voltage samples.
All inputs are finite; a program needn't handle non-finite values.
Results may differ from the reference program's by a relative error of at most 0.0052.
Values may be sent and summed in bfloat16 or wider, within the bound.
No kernel may reach another device: no remote copies, remote signals or barrier semaphores. Data moves between devices by JAX's collectives and lax.ppermute only.
A program may use at most 192 MiB of HBM per device.

```python
import math
import jax
import jax.numpy as jnp
from jax import lax

NFFT = 2048
NCH = 1024
NIN = 1024
TAPS = 12
BLOCK = 8
ITERS = 4
SPECTRA = 192


def with_ends(drawn, own_key, least, high):
    longest = drawn.shape.index(max(drawn.shape))
    spots = []
    for shift in (0, 1):
        where = [jax.random.randint(jax.random.fold_in(own_key, axis), (), 0, length) for axis, length in enumerate(drawn.shape)]
        where[longest] = (where[longest] + shift) % drawn.shape[longest]
        spots.append(tuple(where))
    return drawn.at[spots[0]].set(least).at[spots[1]].set(high)


def centred(rng, extent, scale, limit, held_as=jnp.bfloat16):
    result = scale * jax.random.normal(rng, extent, jnp.float32)
    return jnp.clip(result, min=-limit, max=limit).astype(held_as)


def setup_inputs(seed: int = 0) -> dict:
    keys = jax.random.split(jax.random.key(seed), 4)
    return {
        "voltages": with_ends(jax.random.randint(keys[0], (SPECTRA, NFFT, NIN), -128, 128), jax.random.fold_in(keys[0], 1), -128, 127).astype(jnp.int32),
        "taps": centred(keys[1], (TAPS, NFFT), (TAPS * 16384) ** -0.5, 0.013671875, jnp.float32),
        "start": with_ends(jax.random.randint(keys[2], (BLOCK, 2, NIN), -127, 128), jax.random.fold_in(keys[2], 1), -127, 127).astype(jnp.int32),
    }


def channelize(volt_block, taps):
    frames = volt_block.astype(jnp.float32)
    filtered = jnp.zeros(frames.shape, jnp.float32)
    for tap_index in range(TAPS):
        filtered = filtered + taps[tap_index][None, :, None] * jnp.roll(frames, TAPS - 1 - tap_index, axis=0)
    spectrum = jnp.fft.rfft(filtered, axis=1)[:, :NCH, :] / math.sqrt(NCH)
    paired = jnp.stack([jnp.real(spectrum), jnp.imag(spectrum)], axis=2)
    return jnp.transpose(paired, (1, 0, 2, 3)).astype(jnp.bfloat16)

def clean_channel(spectrum, start_rows):
    highest = lax.Precision.HIGHEST
    channel_data = spectrum.reshape(SPECTRA, 2 * NIN).astype(jnp.float32)
    basis_rows = start_rows
    for iteration in range(ITERS):
        projected = jnp.dot(basis_rows, channel_data.T, precision=highest)
        mapped = jnp.dot(projected, channel_data, precision=highest) / SPECTRA
        gram_matrix = jnp.dot(mapped, mapped.T, precision=highest)
        lower_factor = jnp.linalg.cholesky(gram_matrix)
        basis_rows = lax.linalg.triangular_solve(lower_factor, mapped, left_side=True, lower=True)
    projected = jnp.dot(basis_rows, channel_data.T, precision=highest)
    ritz_matrix = jnp.dot(projected, projected.T, precision=highest) / SPECTRA
    cleaned = channel_data - jnp.dot(projected.T, basis_rows, precision=highest)
    return (cleaned.reshape(SPECTRA, 2, NIN).astype(jnp.bfloat16), ritz_matrix)

def reference(voltages, taps, start):
    block_len = min(NIN, 128)
    block_count = NIN // block_len
    volt_blocks = jnp.transpose(voltages.reshape(SPECTRA, NFFT, block_count, block_len), (2, 0, 1, 3))
    spectra = lax.map(lambda volt_block: channelize(volt_block, taps), volt_blocks)
    spectra = jnp.transpose(spectra, (1, 2, 3, 0, 4)).reshape(NCH, SPECTRA, 2, NIN)
    start_rows = start.reshape(BLOCK, 2 * NIN).astype(jnp.float32)
    cleaned, ritz_matrix = lax.map(lambda spectrum: clean_channel(spectrum, start_rows), spectra)
    return (cleaned, ritz_matrix)
```

```python
import math

import jax
import jax.numpy as jnp
import numpy as np
from jax import lax
from jax.experimental import pallas as pl
from jax.experimental.pallas import tpu as pltpu
from jax.sharding import Mesh, PartitionSpec as P

ITERS = 4
FREQ = ("y", "z", "h")
INP = ("l", "k")
LANES = 128
SLOTS = 3
SHIFT = 5
BF = jnp.bfloat16
F32 = jnp.float32


def cyclic(count, steps):
    return [(i, (i + steps) % count) for i in range(count)]


def split2(value):
    high = lax.reduce_precision(value, 8, 7)
    return high.astype(BF), (value - high).astype(BF)


def dft_tables(frame_len, groups):
    half = frame_len // 2
    per = half // groups
    unit = 2.0 * math.pi / frame_len
    scale = 1.0 / math.sqrt(half)
    n_a = lax.broadcasted_iota(jnp.int32, (groups, half), 1)
    f_a = lax.broadcasted_iota(jnp.int32, (groups, half), 0)
    ang_a = ((f_a * per * n_a) % frame_len).astype(F32) * unit
    n_b = lax.broadcasted_iota(jnp.int32, (per, half), 1)
    j_b = lax.broadcasted_iota(jnp.int32, (per, half), 0)
    ang_b = ((j_b * n_b) % frame_len).astype(F32) * unit
    ca, sa = lax.optimization_barrier((jnp.cos(ang_a), jnp.sin(ang_a)))
    cb, sb = lax.optimization_barrier((jnp.cos(ang_b) * scale, jnp.sin(ang_b) * scale))
    rows = []
    for kind in range(2):
        for par in range(2):
            c2, s2 = cb[par::2][None], sb[par::2][None]
            c1, s1 = ca[:, None], sa[:, None]
            table = c1 * c2 - s1 * s2 if kind == 0 else -(s1 * c2 + c1 * s2)
            rows.append(table.reshape(groups * (per // 2), half))
    return split2(jnp.stack(rows))


def filter_dft_kernel(up, own, down, par, rec, coef, wh, wl, out, fold):
    half = own.shape[2]
    step = 32
    width = SLOTS * LANES

    @pl.when(pl.program_id(0) == 0)
    def _():
        def body(idx, carry):
            rows = pl.ds(pl.multiple_of(idx * step, step), step)
            results = []
            for side in range(2):
                cols = coef[side, rows, :]
                col = lambda t: jnp.broadcast_to(cols[:, t : t + 1], (step, LANES))
                taps = [col(t) for t in range(22)]
                acc = [None] * SLOTS
                for ref, base in ((up, 0), (rec, 19), (own, 6), (par, 14), (down, 12)):
                    for a in range(SLOTS):
                        frame = ref[a, side, rows, :].astype(F32)
                        for r in range(SLOTS):
                            t = base + a - r
                            if base in (0, 12) and not 0 <= t < 12:
                                continue
                            term = taps[t] * frame
                            acc[r] = term if acc[r] is None else acc[r] + term
                results.append(acc)
            for kind in range(2):
                for r in range(SLOTS):
                    lo, hi = results[0][r], results[1][r]
                    value = lo + hi if kind == 0 else lo - hi
                    top = value.astype(BF)
                    rest = (value - top.astype(F32)).astype(BF)
                    fold[kind, rows, r * LANES : (r + 1) * LANES] = top
                    fold[kind, rows, width + r * LANES : width + (r + 1) * LANES] = rest
            return carry

        lax.fori_loop(0, half // step, body, 0)

    groups = out.shape[0]
    for kind in range(2):
        parts = []
        for parity in range(2):
            index = kind * 2 + parity
            full = jnp.dot(wh[index], fold[parity], preferred_element_type=F32)
            rest = jnp.dot(wl[index], fold[parity, :, :width], preferred_element_type=F32)
            total = full[:, :width] + full[:, width:] + rest
            parts.append(total.reshape(groups, total.shape[0] // groups, width))
        both = jnp.concatenate(parts, axis=1).astype(BF)
        out[:, :, kind * width : (kind + 1) * width] = both


def filter_dft(blocks, coef, table_h, table_l, groups):
    frame_len = blocks[0].shape[1]
    half = frame_len // 2
    rows = table_h.shape[1]
    per = half // groups
    width = SLOTS * LANES
    steps = 2
    blocks = [b.reshape(SLOTS, 2, half, LANES) for b in blocks]
    whole = pl.BlockSpec((SLOTS, 2, half, LANES), lambda i: (0, 0, 0, 0))
    table = pl.BlockSpec((4, rows // steps, half), lambda i: (0, i, 0))
    return pl.pallas_call(
        filter_dft_kernel,
        out_shape=jax.ShapeDtypeStruct((groups, per, 2 * width), BF),
        grid=(steps,),
        in_specs=[whole] * 5
        + [pl.BlockSpec((2, half, coef.shape[2]), lambda i: (0, 0, 0)), table, table],
        out_specs=pl.BlockSpec((groups // steps, per, 2 * width), lambda i: (i, 0, 0)),
        scratch_shapes=[pltpu.VMEM((2, half, 2 * width), BF)],
        compiler_params=pltpu.CompilerParams(vmem_limit_bytes=58 << 20),
        name="filter_dft",
    )(*blocks, coef, table_h, table_l)


def split3(value):
    first = value.astype(BF)
    left = value - first.astype(F32)
    second = left.astype(BF)
    third = (left - second.astype(F32)).astype(BF)
    return first, second, third


def wide_dot(a, b, dims):
    return lax.dot_general(
        a, b, (dims, ((), ())), precision=lax.Precision.HIGHEST, preferred_element_type=F32
    )


def iterate_kernel(gram_ref, out, *, spectra):
    count = gram_ref.shape[0]
    block = gram_ref.shape[1] - spectra
    inverse = 1.0 / spectra
    rows = lax.broadcasted_iota(jnp.int32, (block, 1), 0)
    covs = [gram_ref[c, :spectra, :] for c in range(count)]
    proj = [gram_ref[c, spectra:, :] for c in range(count)]
    coef = [None] * count
    for iteration in range(ITERS):
        mapped = [wide_dot(proj[c], covs[c], ((1,), (0,))) * inverse for c in range(count)]
        gram = [wide_dot(mapped[c], proj[c], ((1,), (1,))) * inverse for c in range(count)]
        before = [proj[c] * inverse for c in range(count)]
        scale = [jnp.zeros((block, 1), F32)] * count
        for j in range(block):
            for c in range(count):
                pivot = gram[c][j : j + 1, j : j + 1]
                factor = jnp.where(rows > j, gram[c][:, j : j + 1] / pivot, 0.0)
                scale[c] = jnp.where(rows == j, 1.0 / jnp.sqrt(pivot), scale[c])
                gram[c] = gram[c] - factor * gram[c][j : j + 1, :]
                mapped[c] = mapped[c] - factor * mapped[c][j : j + 1, :]
                before[c] = before[c] - factor * before[c][j : j + 1, :]
        proj = [mapped[c] * scale[c] for c in range(count)]
        coef = [before[c] * scale[c] for c in range(count)]
    for c in range(count):
        out[c, :block, :] = coef[c]
        out[c, block:, :] = wide_dot(coef[c], covs[c], ((1,), (0,)))


def iterate(gram, spectra):
    count, rows, _ = gram.shape
    block = rows - spectra
    return pl.pallas_call(
        lambda g, o: iterate_kernel(g, o, spectra=spectra),
        out_shape=jax.ShapeDtypeStruct((count, 2 * block, spectra), F32),
        compiler_params=pltpu.CompilerParams(vmem_limit_bytes=32 << 20),
        name="iterate",
    )(gram)


def clean_kernel(xa, xb, pair, perm, out, ritz, *, spectra):
    block = pair.shape[1] // 2
    coef = pair[0, :block, :]
    proj = pair[0, block:, :]
    ritz[0] = wide_dot(proj, proj, ((1,), (1,))) * (1.0 / spectra)
    coef3 = jnp.concatenate(split3(coef), axis=0)
    order = perm[...]
    turned = sum(
        jnp.dot(order, part.T, preferred_element_type=F32) for part in split3(proj)
    )
    ph, pm, pt = split3(-turned)
    left = jnp.concatenate([order, ph, ph, ph, pm, pm, pt], axis=1)
    for chunk, ref in enumerate((xa, xb)):
        x = ref[0]
        base = jnp.dot(coef3, x, preferred_element_type=F32)
        base = base[:block] + base[block : 2 * block] + base[2 * block :]
        bh, bm, bt = split3(base)
        right = jnp.concatenate([x, bh, bm, bt, bh, bm, bh], axis=0)
        result = jnp.dot(left, right, preferred_element_type=F32).astype(BF)
        for part in range(2):
            lane = part * 2 * LANES + chunk * LANES
            out[0, :, lane : lane + LANES] = result[:, part * LANES : (part + 1) * LANES]


def clean(xs, pair, spectra):
    channels = pair.shape[0]
    block = pair.shape[1] // 2
    width = 2 * LANES
    order = np.zeros((spectra, spectra), np.float32)
    for m in range(spectra):
        order[m, (m - SHIFT) % spectra] = 1.0
    x_spec = pl.BlockSpec((1, spectra, width), lambda c: (c, 0, 0))
    return pl.pallas_call(
        lambda *refs: clean_kernel(*refs, spectra=spectra),
        out_shape=(
            jax.ShapeDtypeStruct((channels, spectra, 2 * width), BF),
            jax.ShapeDtypeStruct((channels, block, block), F32),
        ),
        grid=(channels,),
        in_specs=[
            x_spec,
            x_spec,
            pl.BlockSpec((1, 2 * block, spectra), lambda c: (c, 0, 0)),
            pl.BlockSpec((spectra, spectra), lambda c: (0, 0)),
        ],
        out_specs=(
            pl.BlockSpec((1, spectra, 2 * width), lambda c: (c, 0, 0)),
            pl.BlockSpec((1, block, block), lambda c: (c, 0, 0)),
        ),
        compiler_params=pltpu.CompilerParams(vmem_limit_bytes=32 << 20),
        name="clean",
    )(*xs, pair, jnp.asarray(order, BF))


def reduce_inputs(gram):
    for axis in ("k", "l"):
        half = gram.shape[0] // 2
        me = lax.axis_index(axis)
        keep = lax.dynamic_slice_in_dim(gram, me * half, half, 0)
        send = lax.dynamic_slice_in_dim(gram, (1 - me) * half, half, 0)
        gram = keep + lax.ppermute(send, axis, cyclic(2, 1))
    return gram


def gather_inputs(value):
    for axis in ("l", "k"):
        value = lax.all_gather(value, axis, tiled=True)
    return value


def shards(voltages, taps, start):
    slots, frame_len, inputs = voltages.shape
    half = frame_len // 2
    block = start.shape[0]
    groups = lax.axis_size("y") * lax.axis_size("z") * 2
    rings = groups // 2
    spectra = groups * slots
    per = half // groups
    chunks = inputs // LANES
    me = lax.axis_index("h")
    frames = voltages.astype(BF)

    by_sample = taps.T
    near = by_sample[:, 1:6]
    far = by_sample[:, 7:12]
    coef = jnp.concatenate(
        [by_sample, jnp.where(me == 0, far, near), jnp.where(me == 0, near, far)], axis=1
    ).reshape(2, half, 22)
    table_h, table_l = dft_tables(frame_len, groups)

    rank = lax.axis_index("l") * 2 + lax.axis_index("k")
    start_local = lax.dynamic_slice_in_dim(start, rank * inputs, inputs, 2).astype(BF)

    xs = []
    gram = None
    last = None
    for chunk in range(chunks):
        own = frames[:, :, chunk * LANES : (chunk + 1) * LANES]
        if last is not None:
            own = lax.optimization_barrier((own,) + last)[0]
        up = lax.ppermute(own, ("y", "z"), cyclic(rings, 1))
        down = lax.ppermute(own, ("y", "z"), cyclic(rings, -1))
        par = lax.ppermute(own, "h", cyclic(2, 1))
        rec = lax.ppermute(jnp.where(me == 0, down, up), "h", cyclic(2, 1))
        last = (up, down)
        spec = filter_dft((up, own, down, par, rec), coef, table_h, table_l, groups)
        turned = lax.all_to_all(spec, FREQ, split_axis=0, concat_axis=0, tiled=True)
        turned = turned.reshape(groups, 2, per // 2, 2, slots, LANES)
        x = turned.transpose(2, 1, 0, 4, 3, 5).reshape(per, spectra, 2 * LANES)
        xs.append(x)
        begin = start_local[:, :, chunk * LANES : (chunk + 1) * LANES].reshape(block, -1)
        square = jnp.einsum("cma,cna->cmn", x, x, preferred_element_type=F32)
        first = jnp.einsum("ka,cma->ckm", begin, x, preferred_element_type=F32)
        part = jnp.concatenate([square, first], axis=1)
        gram = part if gram is None else gram + part
    pair = gather_inputs(iterate(reduce_inputs(gram), spectra))
    cleaned, ritz = clean(xs, pair, spectra)
    return cleaned.reshape(per, spectra, 2, inputs), ritz


def on_mesh(mesh):
    return jax.shard_map(
        shards,
        mesh=mesh,
        in_specs=(P(FREQ, None, INP), P(), P()),
        out_specs=(P(FREQ, None, None, INP), P(FREQ, None, None)),
        check_vma=False,
    )


def solution(mesh):
    freq = mesh.shape["freq"]
    devices = mesh.devices.reshape(freq // 16, 8, 2, 2, 2)
    return on_mesh(Mesh(devices, FREQ + INP))
```

```python
import math

import jax
import jax.numpy as jnp
import numpy as np
from jax import lax
from jax.experimental import pallas as pl
from jax.experimental.pallas import tpu as pltpu
from jax.sharding import Mesh, PartitionSpec as P

ITERS = 4
FREQ = ("y", "z", "h")
INP = ("l", "k")
LANES = 128
SLOTS = 3
SHIFT = 5
BF = jnp.bfloat16
F32 = jnp.float32


def cyclic(count, steps):
    return [(i, (i + steps) % count) for i in range(count)]


def split2(value):
    high = lax.reduce_precision(value, 8, 7)
    return high.astype(BF), (value - high).astype(BF)


def dft_tables(frame_len, groups):
    half = frame_len // 2
    per = half // groups
    unit = 2.0 * math.pi / frame_len
    scale = 1.0 / math.sqrt(half)
    n_a = lax.broadcasted_iota(jnp.int32, (groups, half), 1)
    f_a = lax.broadcasted_iota(jnp.int32, (groups, half), 0)
    ang_a = ((f_a * per * n_a) % frame_len).astype(F32) * unit
    n_b = lax.broadcasted_iota(jnp.int32, (per, half), 1)
    j_b = lax.broadcasted_iota(jnp.int32, (per, half), 0)
    ang_b = ((j_b * n_b) % frame_len).astype(F32) * unit
    ca, sa = lax.optimization_barrier((jnp.cos(ang_a), jnp.sin(ang_a)))
    cb, sb = lax.optimization_barrier((jnp.cos(ang_b) * scale, jnp.sin(ang_b) * scale))
    rows = []
    for par in range(2):
        for kind in range(2):
            c2, s2 = cb[par::2][None], sb[par::2][None]
            c1, s1 = ca[:, None], sa[:, None]
            table = c1 * c2 - s1 * s2 if kind == 0 else -(s1 * c2 + c1 * s2)
            rows.append(table.reshape(groups * (per // 2), half))
    return split2(jnp.stack(rows).reshape(2, half, half))


def filter_kernel(side, up_own, up_rec, own, rec, down_own, down_rec, coef, kept, sent):
    step = 16
    pair = 2 * SLOTS

    def run(first, second, mine):
        def body(idx, carry):
            rows = pl.ds(pl.multiple_of(idx * step, step), step)
            cols = coef[rows, :]
            taps = [jnp.broadcast_to(cols[:, t : t + 1], (step, LANES)) for t in range(12)]
            acc = [None] * pair
            for block in range(3):
                for half in range(2):
                    ref = (first, second)[half][block]
                    for a in range(SLOTS):
                        at = pair * block + SLOTS * half + a
                        frame = ref[a, rows, :].astype(F32)
                        for j in range(pair):
                            t = at - j + SHIFT - 5
                            if 0 <= t < 12:
                                term = taps[t] * frame
                                acc[j] = term if acc[j] is None else acc[j] + term
            for r in range(SLOTS):
                kept[r, rows, :] = acc[SLOTS * mine + r]
                sent[r, rows, :] = acc[SLOTS * (1 - mine) + r]
            return carry

        lax.fori_loop(0, own.shape[1] // step, body, 0, unroll=2)

    mine = (up_own, own, down_own)
    other = (up_rec, rec, down_rec)

    @pl.when(side[0] == 0)
    def _():
        run(mine, other, 0)

    @pl.when(side[0] != 0)
    def _():
        run(other, mine, 1)


def filtered(side, blocks, coef):
    shape = jax.ShapeDtypeStruct(blocks[0].shape, F32)
    in_vmem = pl.BlockSpec(memory_space=pltpu.VMEM)
    return pl.pallas_call(
        filter_kernel,
        out_shape=(shape, shape),
        in_specs=[pl.BlockSpec(memory_space=pltpu.SMEM)] + [in_vmem] * 7,
        out_specs=(in_vmem, in_vmem),
        compiler_params=pltpu.CompilerParams(vmem_limit_bytes=4 << 20),
        cost_estimate=pl.CostEstimate(flops=40_000_000_000, transcendentals=0, bytes_accessed=0),
        name="filter",
    )(side, *blocks, coef)


def dft_kernel(side, own, rec, wh, wl, out, fold):
    half = own.shape[1]
    step = 16
    width = SLOTS * LANES
    sign = jnp.where(side[0] == 0, 1.0, -1.0)

    def body(idx, carry):
        rows = pl.ds(pl.multiple_of(idx * step, step), step)
        for r in range(SLOTS):
            one, two = own[r, rows, :], rec[r, rows, :]
            for parity in range(2):
                value = one + two if parity == 0 else (one - two) * sign
                top = value.astype(BF)
                rest = (value - top.astype(F32)).astype(BF)
                fold[parity, rows, r * LANES : (r + 1) * LANES] = top
                fold[parity, rows, width + r * LANES : width + (r + 1) * LANES] = rest
        return carry

    lax.fori_loop(0, half // step, body, 0, unroll=2)
    groups, per, _ = out.shape
    parts = []
    for parity in range(2):
        full = jnp.dot(wh[parity], fold[parity], preferred_element_type=F32)
        rest = jnp.dot(wl[parity], fold[parity, :, :width], preferred_element_type=F32)
        total = full[:, :width] + full[:, width:] + rest
        parts.append(total.reshape(2, groups, per // 2, width))
    for kind in range(2):
        both = jnp.concatenate([parts[0][kind], parts[1][kind]], axis=1).astype(BF)
        out[:, :, kind * width : (kind + 1) * width] = both


def dft(side, own, rec, table_h, table_l, groups):
    half = own.shape[1]
    width = SLOTS * LANES
    in_vmem = pl.BlockSpec(memory_space=pltpu.VMEM)
    return pl.pallas_call(
        dft_kernel,
        out_shape=jax.ShapeDtypeStruct((groups, half // groups, 2 * width), BF),
        in_specs=[pl.BlockSpec(memory_space=pltpu.SMEM)] + [in_vmem] * 4,
        out_specs=in_vmem,
        scratch_shapes=[pltpu.VMEM((2, half, 2 * width), BF)],
        compiler_params=pltpu.CompilerParams(vmem_limit_bytes=16 << 20),
        cost_estimate=pl.CostEstimate(flops=40_000_000_000, transcendentals=0, bytes_accessed=0),
        name="dft",
    )(side, own, rec, table_h, table_l)


NT = (((1,), (1,)), ((), ()))


def gram_kernel(place, turned, begin, order, *refs):
    before = refs[0] if len(refs) == 3 else None
    x_out, packed = refs[-2:]
    groups, per, _ = turned.shape
    spectra = x_out.shape[1]
    block = begin.shape[0]
    tile = order.shape[0] // per
    for base in range(0, groups, tile):
        rows = turned[base : base + tile].reshape(tile * per, -1)
        rows = jnp.dot(order[...], rows, preferred_element_type=F32).astype(BF)
        for c in range(per):
            for part in range(2):
                for r in range(SLOTS):
                    lane = (part * SLOTS + r) * LANES
                    at = r * groups + base
                    x_out[c, at : at + tile, part * LANES : (part + 1) * LANES] = rows[
                        c * tile : (c + 1) * tile, lane : lane + LANES
                    ]
    cut = min(spectra, LANES)
    tail = spectra - cut
    quarter = per // 4
    dot = lambda a, b: lax.dot_general(a, b, NT, preferred_element_type=F32)
    for c in range(per):
        top = (c // (2 * quarter) + place[0]) % 2
        low = ((c // quarter) % 2 + place[1]) % 2
        pos = top * (2 * quarter) + low * quarter + c % quarter

        def put(r0, r1, l0, l1, value):
            if before is not None:
                value = value + before[pos, r0:r1, l0:l1]
            packed[pos, r0:r1, l0:l1] = value

        x = x_out[c]
        put(0, spectra, 0, cut, dot(x, x[:cut]))
        first = dot(begin[...], x)
        at = spectra + tail // 2
        put(at, at + block, 0, cut, first[:, :cut])
        if tail:
            corner = dot(x[cut:], x[cut:])
            put(spectra, at, 0, tail, corner[: tail // 2])
            put(spectra, at, tail, 2 * tail, corner[tail // 2 :])
            put(at + block, at + 2 * block, 0, tail, first[:, cut:])


def packed_rows(spectra, block):
    return spectra + max(spectra - LANES, 0) // 2 + 2 * block


def gram(place, turned, begin, before):
    groups, per, _ = turned.shape
    spectra = groups * SLOTS
    block = begin.shape[0]
    tile = min(16, groups)
    order = np.zeros((per, tile, tile, per), np.float32)
    for c in range(per):
        for src in range(tile):
            order[c, src, src, (c % 2) * (per // 2) + c // 2] = 1.0
    order = jnp.asarray(order.reshape(per * tile, per * tile), BF)
    in_vmem = pl.BlockSpec(memory_space=pltpu.VMEM)
    operands = [turned, begin, order] + ([] if before is None else [before])
    return pl.pallas_call(
        gram_kernel,
        out_shape=(
            jax.ShapeDtypeStruct((per, spectra, 2 * LANES), BF),
            jax.ShapeDtypeStruct((per, packed_rows(spectra, block), LANES), F32),
        ),
        in_specs=[pl.BlockSpec(memory_space=pltpu.SMEM)] + [in_vmem] * len(operands),
        out_specs=(in_vmem, in_vmem),
        compiler_params=pltpu.CompilerParams(vmem_limit_bytes=10 << 20),
        cost_estimate=pl.CostEstimate(flops=10_000_000_000, transcendentals=0, bytes_accessed=0),
        name="gram",
    )(place, *operands)


def split3(value):
    first = value.astype(BF)
    left = value - first.astype(F32)
    second = left.astype(BF)
    third = (left - second.astype(F32)).astype(BF)
    return first, second, third


def wide_dot(a, b, dims):
    return lax.dot_general(
        a, b, (dims, ((), ())), precision=lax.Precision.HIGHEST, preferred_element_type=F32
    )


def unpack(packed, spectra, block):
    cut = min(spectra, LANES)
    tail = spectra - cut
    square = packed[:spectra, :cut]
    if not tail:
        return square, packed[spectra : spectra + block, :cut]
    at = spectra + tail // 2
    corner = packed[spectra:at, : 2 * tail]
    corner = jnp.concatenate([corner[:, :tail], corner[:, tail:]], axis=0)
    side = jnp.concatenate([square[cut:].T, corner], axis=0)
    first = jnp.concatenate(
        [packed[at : at + block, :cut], packed[at + block : at + 2 * block, :tail]], axis=1
    )
    return jnp.concatenate([square, side], axis=1), first


def iterate_kernel(gram_ref, out, *, spectra):
    count = gram_ref.shape[0]
    block = out.shape[1] // 2
    inverse = 1.0 / spectra
    rows = lax.broadcasted_iota(jnp.int32, (block, 1), 0)
    both = [unpack(gram_ref[c], spectra, block) for c in range(count)]
    covs = [pair[0] for pair in both]
    proj = [pair[1] for pair in both]
    coef = [None] * count
    for iteration in range(ITERS):
        mapped = [wide_dot(proj[c], covs[c], ((1,), (0,))) * inverse for c in range(count)]
        gram = [wide_dot(mapped[c], proj[c], ((1,), (1,))) * inverse for c in range(count)]
        before = [proj[c] * inverse for c in range(count)]
        scale = [jnp.zeros((block, 1), F32)] * count
        for j in range(block):
            for c in range(count):
                pivot = gram[c][j : j + 1, j : j + 1]
                factor = jnp.where(rows > j, gram[c][:, j : j + 1] / pivot, 0.0)
                scale[c] = jnp.where(rows == j, 1.0 / jnp.sqrt(pivot), scale[c])
                gram[c] = gram[c] - factor * gram[c][j : j + 1, :]
                mapped[c] = mapped[c] - factor * mapped[c][j : j + 1, :]
                before[c] = before[c] - factor * before[c][j : j + 1, :]
        proj = [mapped[c] * scale[c] for c in range(count)]
        coef = [before[c] * scale[c] for c in range(count)]
    for c in range(count):
        out[c, :block, :] = coef[c]
        out[c, block:, :] = wide_dot(coef[c], covs[c], ((1,), (0,)))


def iterate(gram, spectra, block):
    count = gram.shape[0]
    return pl.pallas_call(
        lambda g, o: iterate_kernel(g, o, spectra=spectra),
        out_shape=jax.ShapeDtypeStruct((count, 2 * block, spectra), F32),
        compiler_params=pltpu.CompilerParams(vmem_limit_bytes=12 << 20),
        name="iterate",
    )(gram)


def clean_kernel(xa, xb, pair, perm, out, ritz):
    count, spectra, _ = xa.shape
    block = pair.shape[1] // 2
    order = perm[...]
    for c in range(count):
        coef = pair[c, :block, :]
        proj = pair[c, block:, :]
        ritz[c] = wide_dot(proj, proj, NT[0]) * (1.0 / spectra)
        coef3 = jnp.concatenate(split3(coef), axis=0)
        proj3 = jnp.concatenate(split3(proj), axis=0)
        turned = lax.dot_general(order, proj3, NT, preferred_element_type=F32)
        ph, pm, pt = [(-turned[:, i * block : (i + 1) * block]).astype(BF) for i in range(3)]
        left = jnp.concatenate([order, ph, ph, ph, pm, pm, pt], axis=1)
        for chunk, ref in enumerate((xa, xb)):
            x = ref[c]
            base = jnp.dot(coef3, x, preferred_element_type=F32)
            base = base[:block] + base[block : 2 * block] + base[2 * block :]
            bh, bm, bt = split3(base)
            right = jnp.concatenate([x, bh, bm, bt, bh, bm, bh], axis=0)
            result = jnp.dot(left, right, preferred_element_type=F32).astype(BF)
            for part in range(2):
                lane = part * 2 * LANES + chunk * LANES
                out[c, :, lane : lane + LANES] = result[:, part * LANES : (part + 1) * LANES]


def clean(xs, pair, spectra):
    channels = pair.shape[0]
    block = pair.shape[1] // 2
    width = 2 * LANES
    step = 4
    order = np.zeros((spectra, spectra), np.float32)
    groups = spectra // SLOTS
    for src in range(groups):
        for r in range(SLOTS):
            order[(SLOTS * src + r + SHIFT) % spectra, r * groups + src] = 1.0
    x_spec = pl.BlockSpec((step, spectra, width), lambda c: (c, 0, 0))
    return pl.pallas_call(
        clean_kernel,
        out_shape=(
            jax.ShapeDtypeStruct((channels, spectra, 2 * width), BF),
            jax.ShapeDtypeStruct((channels, block, block), F32),
        ),
        grid=(channels // step,),
        in_specs=[
            x_spec,
            x_spec,
            pl.BlockSpec((step, 2 * block, spectra), lambda c: (c, 0, 0)),
            pl.BlockSpec((spectra, spectra), lambda c: (0, 0)),
        ],
        out_specs=(
            pl.BlockSpec((step, spectra, 2 * width), lambda c: (c, 0, 0)),
            pl.BlockSpec((step, block, block), lambda c: (c, 0, 0)),
        ),
        compiler_params=pltpu.CompilerParams(vmem_limit_bytes=12 << 20),
        name="clean",
    )(*xs, pair, jnp.asarray(order, BF))


def reduce_inputs(packed):
    for axis in ("k", "l"):
        half = packed.shape[0] // 2
        packed = packed[:half] + lax.ppermute(packed[half:], axis, cyclic(2, 1))
    return packed


def gather_inputs(value):
    for axis in ("l", "k"):
        value = lax.all_gather(value, axis, tiled=True)
    return value


def shards(voltages, taps, start):
    slots, frame_len, inputs = voltages.shape
    half = frame_len // 2
    block = start.shape[0]
    groups = lax.axis_size("y") * lax.axis_size("z") * 2
    rings = groups // 2
    spectra = groups * slots
    per = half // groups
    chunks = inputs // LANES
    me = lax.axis_index("h")
    side = me.reshape(1)
    k_index, l_index = lax.axis_index("k"), lax.axis_index("l")
    coef = lax.dynamic_slice_in_dim(taps.T, me * half, half, 0)
    table_h, table_l = dft_tables(frame_len, groups)

    def piece(chunk, which):
        at = (0, which * half, chunk * LANES)
        return lax.dynamic_slice(voltages, at, (slots, half, LANES)).astype(BF)

    def swap(value):
        return lax.ppermute(value, "h", cyclic(2, 1))

    def both_ways(value):
        return (
            lax.ppermute(value, ("y", "z"), cyclic(rings, 1)),
            lax.ppermute(value, ("y", "z"), cyclic(rings, -1)),
        )

    rank = l_index * 2 + k_index
    begin = lax.dynamic_slice_in_dim(start, rank * inputs, inputs, 2).astype(BF)
    begin = begin.reshape(block, 2, chunks, LANES).transpose(2, 0, 1, 3).reshape(chunks, block, -1)

    sums = []
    gate_x = gate_z = None
    for chunk in range(chunks):
        own, send = piece(chunk, me), piece(chunk, 1 - me)
        if gate_x is not None:
            own, send, _ = lax.optimization_barrier((own, send, gate_x))
        rec = swap(send)
        gate_x = rec
        moving = (own, rec)
        if gate_z is not None:
            moving = lax.optimization_barrier((own, rec) + gate_z)[:2]
        up_own, down_own = both_ways(moving[0])
        up_rec, down_rec = both_ways(moving[1])
        gate_z = (up_rec, down_rec)
        blocks = (up_own, up_rec, own, rec, down_own, down_rec)
        if chunk == 0:
            blocks, (table_h, table_l) = lax.optimization_barrier((blocks, (table_h, table_l)))
        sums.append(filtered(side, blocks, coef))
    turned = []
    for chunk in range(chunks):
        kept, sent = sums[chunk]
        back = swap(sent)
        if chunk + 1 < chunks:
            kept, back, later = lax.optimization_barrier((kept, back, sums[chunk + 1]))
            sums[chunk + 1] = later
        spec = dft(side, kept, back, table_h, table_l, groups)
        turned.append(lax.all_to_all(spec, FREQ, split_axis=0, concat_axis=0, tiled=True))
    place = jnp.stack([k_index, l_index])
    xs, packed = [], None
    for chunk in range(chunks):
        x, packed = gram(place, turned[chunk], begin[chunk], packed)
        xs.append(x)
    pair = gather_inputs(iterate(reduce_inputs(packed), spectra, block))
    cleaned, ritz = clean(xs, pair, spectra)
    return cleaned.reshape(per, spectra, 2, inputs), ritz


def on_mesh(mesh):
    return jax.shard_map(
        shards,
        mesh=mesh,
        in_specs=(P(FREQ, None, INP), P(), P()),
        out_specs=(P(FREQ, None, None, INP), P(FREQ, None, None)),
        check_vma=False,
    )


def solution(mesh):
    freq = mesh.shape["freq"]
    devices = mesh.devices.reshape(freq // 16, 8, 2, 2, 2)
    return on_mesh(Mesh(devices, FREQ + INP))
```

```python
import functools
import math

import jax
import jax.numpy as jnp
import numpy as np
from jax import lax
from jax.experimental import pallas as pl
from jax.experimental.pallas import tpu as pltpu
from jax.sharding import Mesh, PartitionSpec as P

ITERS = 4
FREQ = ("y", "z", "h")
INP = ("l", "k")
LANES = 128
SLOTS = 3
SHIFT = 5
BF = jnp.bfloat16
F32 = jnp.float32
FILTER_HINT = 40_000_000_000
DFT_HINT = 40_000_000_000


def cyclic(count, steps):
    return [(i, (i + steps) % count) for i in range(count)]


def split2(value):
    high = lax.reduce_precision(value, 8, 7)
    return high.astype(BF), (value - high).astype(BF)


def dft_tables(frame_len, groups):
    half = frame_len // 2
    per = half // groups
    unit = 2.0 * math.pi / frame_len
    scale = 1.0 / math.sqrt(half)
    n_a = lax.broadcasted_iota(jnp.int32, (groups, half), 1)
    f_a = lax.broadcasted_iota(jnp.int32, (groups, half), 0)
    ang_a = ((f_a * per * n_a) % frame_len).astype(F32) * unit
    n_b = lax.broadcasted_iota(jnp.int32, (per, half), 1)
    j_b = lax.broadcasted_iota(jnp.int32, (per, half), 0)
    ang_b = ((j_b * n_b) % frame_len).astype(F32) * unit
    ca, sa = lax.optimization_barrier((jnp.cos(ang_a), jnp.sin(ang_a)))
    cb, sb = lax.optimization_barrier((jnp.cos(ang_b) * scale, jnp.sin(ang_b) * scale))
    rows = []
    for par in range(2):
        for kind in range(2):
            c2, s2 = cb[par::2][None], sb[par::2][None]
            c1, s1 = ca[:, None], sa[:, None]
            table = c1 * c2 - s1 * s2 if kind == 0 else -(s1 * c2 + c1 * s2)
            rows.append(table.reshape(groups * (per // 2), half))
    return split2(jnp.stack(rows).reshape(2, half, half))


def filter_kernel(side, coef, *refs, views):
    kept, sent = refs[-2:]
    step = 16
    pair = 2 * SLOTS

    def load(view, a, rows):
        ref, lead, offset = refs[view[0]], view[1], view[2]
        rows = pl.ds(rows + offset, step)
        value = ref[a, rows, :] if lead is None else ref[lead, a, rows, :]
        return value.astype(F32)

    def run(first, second, mine):
        def body(idx, carry):
            start = pl.multiple_of(idx * step, step)
            rows = pl.ds(start, step)
            cols = coef[rows, :]
            taps = [jnp.broadcast_to(cols[:, t : t + 1], (step, LANES)) for t in range(12)]
            acc = [None] * pair
            for block in range(3):
                for half in range(2):
                    view = (first, second)[half][block]
                    for a in range(SLOTS):
                        at = pair * block + SLOTS * half + a
                        frame = load(view, a, start)
                        for j in range(pair):
                            t = at - j + SHIFT - 5
                            if 0 <= t < 12:
                                term = taps[t] * frame
                                acc[j] = term if acc[j] is None else acc[j] + term
            for r in range(SLOTS):
                kept[r, rows, :] = acc[SLOTS * mine + r]
                sent[r, rows, :] = acc[SLOTS * (1 - mine) + r]
            return carry

        lax.fori_loop(0, kept.shape[1] // step, body, 0, unroll=2)

    own, rec = views[:3], views[3:]

    @pl.when(side[0] == 0)
    def _():
        run(own, rec, 0)

    @pl.when(side[0] != 0)
    def _():
        run(rec, own, 1)


def filtered(side, arrays, views, coef):
    shape = jax.ShapeDtypeStruct((SLOTS, coef.shape[0], LANES), F32)
    in_vmem = pl.BlockSpec(memory_space=pltpu.VMEM)
    return pl.pallas_call(
        functools.partial(filter_kernel, views=views),
        out_shape=(shape, shape),
        in_specs=[pl.BlockSpec(memory_space=pltpu.SMEM)] + [in_vmem] * (1 + len(arrays)),
        out_specs=(in_vmem, in_vmem),
        compiler_params=pltpu.CompilerParams(vmem_limit_bytes=4 << 20),
        cost_estimate=pl.CostEstimate(flops=FILTER_HINT, transcendentals=0, bytes_accessed=0),
        name="filter",
    )(side, coef, *arrays)


def dft_kernel(side, *refs):
    subs = (len(refs) - 5) // 2
    owns, recs = refs[:subs], refs[subs : 2 * subs]
    wh, wl, out, fold, even = refs[2 * subs :]
    tile = 16
    width = SLOTS * LANES
    groups, per, _ = out.shape
    sign = jnp.where(side[0] == 0, 1.0, -1.0)
    step = pl.program_id(0)

    @pl.when(step == 0)
    def _():
        first = 0
        for sub in range(subs):
            size = owns[sub].shape[1]

            def body(idx, carry):
                start = pl.multiple_of(idx * tile, tile)
                rows = pl.ds(start, tile)
                at = pl.ds(start + first, tile)
                for r in range(SLOTS):
                    one, two = owns[sub][r, rows, :], recs[sub][r, rows, :]
                    for par in range(2):
                        value = one + two if par == 0 else (one - two) * sign
                        top = value.astype(BF)
                        rest = (value - top.astype(F32)).astype(BF)
                        fold[par, at, r * LANES : (r + 1) * LANES] = top
                        fold[par, at, width + r * LANES : width + (r + 1) * LANES] = rest
                return carry

            lax.fori_loop(0, size // tile, body, 0, unroll=2)
            first += size

    data = fold.at[step // 2]
    full = jnp.dot(wh[0], data[...], preferred_element_type=F32)
    rest = jnp.dot(wl[0], data[:, :width], preferred_element_type=F32)
    total = (full[:, :width] + full[:, width:] + rest).reshape(groups, per // 2, width)

    @pl.when(step < 2)
    def _():
        even[step] = total

    for kind in range(2):

        @pl.when(step == 2 + kind)
        def _():
            both = jnp.concatenate([even[kind], total], axis=1).astype(BF)
            out[:, :, kind * width : (kind + 1) * width] = both


def dft(side, owns, recs, table_h, table_l, groups, room):
    half = table_h.shape[1]
    per = half // groups
    width = SLOTS * LANES
    table = pl.BlockSpec((1, half // 2, half), lambda i: (i // 2, i % 2, 0))
    return pl.pallas_call(
        dft_kernel,
        out_shape=jax.ShapeDtypeStruct((groups, per, 2 * width), BF),
        grid=(4,),
        in_specs=[pl.BlockSpec(memory_space=pltpu.SMEM)]
        + [pl.BlockSpec(value.shape, lambda i: (0, 0, 0)) for value in owns + recs]
        + [table, table],
        out_specs=pl.BlockSpec((groups, per, 2 * width), lambda i: (0, 0, 0)),
        scratch_shapes=[
            pltpu.VMEM((2, half, 2 * width), BF),
            pltpu.VMEM((2, groups, per // 2, width), F32),
        ],
        compiler_params=pltpu.CompilerParams(vmem_limit_bytes=room << 20),
        cost_estimate=pl.CostEstimate(flops=DFT_HINT, transcendentals=0, bytes_accessed=0),
        name="dft",
    )(side, *owns, *recs, table_h, table_l)


NT = (((1,), (1,)), ((), ()))


def gram_kernel(place, turned, begin, order, *refs):
    before = refs[0] if len(refs) == 3 else None
    x_out, packed = refs[-2:]
    groups, per, _ = turned.shape
    spectra = x_out.shape[1]
    block = begin.shape[0]
    tile = order.shape[0] // per
    for base in range(0, groups, tile):
        rows = turned[base : base + tile].reshape(tile * per, -1)
        rows = jnp.dot(order[...], rows, preferred_element_type=F32).astype(BF)
        for c in range(per):
            for part in range(2):
                for r in range(SLOTS):
                    lane = (part * SLOTS + r) * LANES
                    at = r * groups + base
                    x_out[c, at : at + tile, part * LANES : (part + 1) * LANES] = rows[
                        c * tile : (c + 1) * tile, lane : lane + LANES
                    ]
    cut = min(spectra, LANES)
    tail = spectra - cut
    quarter = per // 4
    dot = lambda a, b: lax.dot_general(a, b, NT, preferred_element_type=F32)
    for c in range(per):
        top = (c // (2 * quarter) + place[0]) % 2
        low = ((c // quarter) % 2 + place[1]) % 2
        pos = top * (2 * quarter) + low * quarter + c % quarter

        def put(r0, r1, l0, l1, value):
            if before is not None:
                value = value + before[pos, r0:r1, l0:l1]
            packed[pos, r0:r1, l0:l1] = value

        x = x_out[c]
        put(0, spectra, 0, cut, dot(x, x[:cut]))
        first = dot(begin[...], x)
        at = spectra + tail // 2
        put(at, at + block, 0, cut, first[:, :cut])
        if tail:
            corner = dot(x[cut:], x[cut:])
            put(spectra, at, 0, tail, corner[: tail // 2])
            put(spectra, at, tail, 2 * tail, corner[tail // 2 :])
            put(at + block, at + 2 * block, 0, tail, first[:, cut:])


def packed_rows(spectra, block):
    return spectra + max(spectra - LANES, 0) // 2 + 2 * block


def gram(place, turned, begin, before):
    groups, per, _ = turned.shape
    spectra = groups * SLOTS
    block = begin.shape[0]
    tile = min(16, groups)
    order = np.zeros((per, tile, tile, per), np.float32)
    for c in range(per):
        for src in range(tile):
            order[c, src, src, (c % 2) * (per // 2) + c // 2] = 1.0
    order = jnp.asarray(order.reshape(per * tile, per * tile), BF)
    in_vmem = pl.BlockSpec(memory_space=pltpu.VMEM)
    operands = [turned, begin, order] + ([] if before is None else [before])
    return pl.pallas_call(
        gram_kernel,
        out_shape=(
            jax.ShapeDtypeStruct((per, spectra, 2 * LANES), BF),
            jax.ShapeDtypeStruct((per, packed_rows(spectra, block), LANES), F32),
        ),
        in_specs=[pl.BlockSpec(memory_space=pltpu.SMEM)] + [in_vmem] * len(operands),
        out_specs=(in_vmem, in_vmem),
        compiler_params=pltpu.CompilerParams(vmem_limit_bytes=10 << 20),
        cost_estimate=pl.CostEstimate(flops=10_000_000_000, transcendentals=0, bytes_accessed=0),
        name="gram",
    )(place, *operands)


def split3(value):
    first = value.astype(BF)
    left = value - first.astype(F32)
    second = left.astype(BF)
    third = (left - second.astype(F32)).astype(BF)
    return first, second, third


def wide_dot(a, b, dims):
    return lax.dot_general(
        a, b, (dims, ((), ())), precision=lax.Precision.HIGHEST, preferred_element_type=F32
    )


def unpack(packed, spectra, block):
    cut = min(spectra, LANES)
    tail = spectra - cut
    square = packed[:spectra, :cut]
    if not tail:
        return square, packed[spectra : spectra + block, :cut]
    at = spectra + tail // 2
    corner = packed[spectra:at, : 2 * tail]
    corner = jnp.concatenate([corner[:, :tail], corner[:, tail:]], axis=0)
    side = jnp.concatenate([square[cut:].T, corner], axis=0)
    first = jnp.concatenate(
        [packed[at : at + block, :cut], packed[at + block : at + 2 * block, :tail]], axis=1
    )
    return jnp.concatenate([square, side], axis=1), first


def iterate_kernel(gram_ref, out, *, spectra):
    count = gram_ref.shape[0]
    block = out.shape[1] // 2
    inverse = 1.0 / spectra
    rows = lax.broadcasted_iota(jnp.int32, (block, 1), 0)
    both = [unpack(gram_ref[c], spectra, block) for c in range(count)]
    covs = [split3(pair[0]) for pair in both]

    def times(value, parts):
        a, b, c = split3(value)
        lead = jnp.dot(jnp.concatenate([a, b, c], axis=0), parts[0], preferred_element_type=F32)
        next_ = jnp.dot(jnp.concatenate([a, b], axis=0), parts[1], preferred_element_type=F32)
        last = jnp.dot(a, parts[2], preferred_element_type=F32)
        small = lead[2 * block :] + next_[block:] + last
        return lead[:block] + (lead[block : 2 * block] + next_[:block] + small)

    proj = [pair[1] for pair in both]
    coef = [None] * count
    for iteration in range(ITERS):
        mapped = [times(proj[c], covs[c]) * inverse for c in range(count)]
        gram = [wide_dot(mapped[c], proj[c], ((1,), (1,))) * inverse for c in range(count)]
        before = [proj[c] * inverse for c in range(count)]
        scale = [jnp.zeros((block, 1), F32)] * count
        for j in range(block):
            for c in range(count):
                pivot = gram[c][j : j + 1, j : j + 1]
                factor = jnp.where(rows > j, gram[c][:, j : j + 1] / pivot, 0.0)
                scale[c] = jnp.where(rows == j, 1.0 / jnp.sqrt(pivot), scale[c])
                gram[c] = gram[c] - factor * gram[c][j : j + 1, :]
                mapped[c] = mapped[c] - factor * mapped[c][j : j + 1, :]
                if iteration == ITERS - 1:
                    before[c] = before[c] - factor * before[c][j : j + 1, :]
        proj = [mapped[c] * scale[c] for c in range(count)]
        coef = [before[c] * scale[c] for c in range(count)]
    for c in range(count):
        out[c, :block, :] = coef[c]
        out[c, block:, :] = times(coef[c], covs[c])


def iterate(gram, spectra, block):
    count = gram.shape[0]
    return pl.pallas_call(
        lambda g, o: iterate_kernel(g, o, spectra=spectra),
        out_shape=jax.ShapeDtypeStruct((count, 2 * block, spectra), F32),
        compiler_params=pltpu.CompilerParams(vmem_limit_bytes=12 << 20),
        name="iterate",
    )(gram)


def clean_kernel(xa, xb, pair, perm, out, ritz):
    count, spectra, _ = xa.shape
    block = pair.shape[1] // 2
    order = perm[...]
    for c in range(count):
        coef = pair[c, :block, :]
        proj = pair[c, block:, :]
        ritz[c] = wide_dot(proj, proj, NT[0]) * (1.0 / spectra)
        coef3 = jnp.concatenate(split3(coef), axis=0)
        proj3 = jnp.concatenate(split3(proj), axis=0)
        turned = lax.dot_general(order, proj3, NT, preferred_element_type=F32)
        ph, pm, pt = [(-turned[:, i * block : (i + 1) * block]).astype(BF) for i in range(3)]
        left = jnp.concatenate([order, ph, ph, ph, pm, pm, pt], axis=1)
        for chunk, ref in enumerate((xa, xb)):
            x = ref[c]
            base = jnp.dot(coef3, x, preferred_element_type=F32)
            base = base[:block] + base[block : 2 * block] + base[2 * block :]
            bh, bm, bt = split3(base)
            right = jnp.concatenate([x, bh, bm, bt, bh, bm, bh], axis=0)
            result = jnp.dot(left, right, preferred_element_type=F32).astype(BF)
            for part in range(2):
                lane = part * 2 * LANES + chunk * LANES
                out[c, :, lane : lane + LANES] = result[:, part * LANES : (part + 1) * LANES]


def clean(xs, pair, spectra):
    channels = pair.shape[0]
    block = pair.shape[1] // 2
    width = 2 * LANES
    step = 4
    order = np.zeros((spectra, spectra), np.float32)
    groups = spectra // SLOTS
    for src in range(groups):
        for r in range(SLOTS):
            order[(SLOTS * src + r + SHIFT) % spectra, r * groups + src] = 1.0
    x_spec = pl.BlockSpec((step, spectra, width), lambda c: (c, 0, 0))
    return pl.pallas_call(
        clean_kernel,
        out_shape=(
            jax.ShapeDtypeStruct((channels, spectra, 2 * width), BF),
            jax.ShapeDtypeStruct((channels, block, block), F32),
        ),
        grid=(channels // step,),
        in_specs=[
            x_spec,
            x_spec,
            pl.BlockSpec((step, 2 * block, spectra), lambda c: (c, 0, 0)),
            pl.BlockSpec((spectra, spectra), lambda c: (0, 0)),
        ],
        out_specs=(
            pl.BlockSpec((step, spectra, 2 * width), lambda c: (c, 0, 0)),
            pl.BlockSpec((step, block, block), lambda c: (c, 0, 0)),
        ),
        compiler_params=pltpu.CompilerParams(vmem_limit_bytes=12 << 20),
        name="clean",
    )(*xs, pair, jnp.asarray(order, BF))


def reduce_inputs(packed):
    for axis in ("k", "l"):
        half = packed.shape[0] // 2
        packed = packed[:half] + lax.ppermute(packed[half:], axis, cyclic(2, 1))
    return packed


def gather_inputs(value):
    for axis in ("l", "k"):
        value = lax.all_gather(value, axis, tiled=True)
    return value


def shards(voltages, taps, start):
    slots, frame_len, inputs = voltages.shape
    half = frame_len // 2
    block = start.shape[0]
    groups = lax.axis_size("y") * lax.axis_size("z") * 2
    rings = groups // 2
    spectra = groups * slots
    per = half // groups
    chunks = inputs // LANES
    me = lax.axis_index("h")
    side = me.reshape(1)
    k_index, l_index = lax.axis_index("k"), lax.axis_index("l")
    coef = lax.dynamic_slice_in_dim(taps.T, me * half, half, 0)
    table_h, table_l = dft_tables(frame_len, groups)

    def piece(chunk, which, first, size):
        at = (0, which * half + first, chunk * LANES)
        return lax.dynamic_slice(voltages, at, (slots, size, LANES)).astype(BF)

    def swap(value):
        return lax.ppermute(value, "h", cyclic(2, 1))

    def both_ways(value):
        return (
            lax.ppermute(value, ("y", "z"), cyclic(rings, 1)),
            lax.ppermute(value, ("y", "z"), cyclic(rings, -1)),
        )

    rank = l_index * 2 + k_index
    begin = lax.dynamic_slice_in_dim(start, rank * inputs, inputs, 2).astype(BF)
    begin = begin.reshape(block, 2, chunks, LANES).transpose(2, 0, 1, 3).reshape(chunks, block, -1)

    fence = lax.optimization_barrier
    sub = half // 2
    cut = half * 8 // 16
    coefs = [coef[:sub], coef[sub:]]
    coefs_b = [coef[:cut], coef[cut:]]
    parts_b = ((0, cut), (cut, half - cut))

    own_a = piece(0, me, 0, half)
    send_a = [piece(0, 1 - me, i * sub, sub) for i in range(2)]
    up_own, down_own = both_ways(own_a)
    rec_a = [swap(send_a[0])]
    rec_a.append(swap(fence((send_a[1], rec_a[0]))[0]))
    ways_a = [both_ways(value) for value in rec_a]
    own_b = [piece(1, me, *part) for part in parts_b]
    rec_b = []
    for i in range(2):
        rec_b.append(swap(fence((piece(1, 1 - me, *parts_b[i]), rec_a[1]))[0]))
    both_b = [jnp.stack([own_b[i], rec_b[i]]) for i in range(2)]
    ways_b = [both_ways(fence((both_b[i], ways_a[i]))[0]) for i in range(2)]

    kept, back = [[], []], [[], []]
    for i in range(2):
        arrays = (up_own, own_a, down_own, ways_a[i][0], rec_a[i], ways_a[i][1])
        views = tuple((n, None, i * sub if n < 3 else 0) for n in range(6))
        if i == 0:
            arrays, (table_h, table_l) = fence((arrays, (table_h, table_l)))
        mine, sent = filtered(side, arrays, views, coefs[i])
        kept[0].append(mine)
        back[0].append(swap(sent))
    specs = []
    for i in range(2):
        arrays = (ways_b[i][0], both_b[i], ways_b[i][1])
        views = tuple((n % 3, n // 3, 0) for n in range(6))
        if i == 1:
            specs.append(dft(side, kept[0], back[0], table_h, table_l, groups, 30))
        mine, sent = filtered(side, arrays, views, coefs_b[i])
        kept[1].append(mine)
        if i == 0:
            kept[0], back[0], sent = fence((kept[0], back[0], sent))
        back[1].append(swap(sent))
    specs.append(dft(side, kept[1], back[1], table_h, table_l, groups, 58))
    turned = [lax.all_to_all(spec, FREQ, split_axis=0, concat_axis=0, tiled=True) for spec in specs]
    place = jnp.stack([k_index, l_index])
    xs, packed = [], None
    for chunk in range(chunks):
        x, packed = gram(place, turned[chunk], begin[chunk], packed)
        xs.append(x)
    pair = gather_inputs(iterate(reduce_inputs(packed), spectra, block))
    cleaned, ritz = clean(xs, pair, spectra)
    return cleaned.reshape(per, spectra, 2, inputs), ritz


def on_mesh(mesh):
    return jax.shard_map(
        shards,
        mesh=mesh,
        in_specs=(P(FREQ, None, INP), P(), P()),
        out_specs=(P(FREQ, None, None, INP), P(FREQ, None, None)),
        check_vma=False,
    )


def solution(mesh):
    freq = mesh.shape["freq"]
    devices = mesh.devices.reshape(freq // 16, 8, 2, 2, 2)
    return on_mesh(Mesh(devices, FREQ + INP))
```

```python
import functools
import math

import jax
import jax.numpy as jnp
import numpy as np
from jax import lax
from jax.experimental import pallas as pl
from jax.experimental.pallas import tpu as pltpu
from jax.sharding import Mesh, PartitionSpec as P

ITERS = 4
FREQ = ("y", "z", "h")
INP = ("l", "k")
LANES = 128
SLOTS = 3
SHIFT = 5
BF = jnp.bfloat16
F32 = jnp.float32
FILTER_HINT = 40_000_000_000
DFT_HINT = 40_000_000_000


def cyclic(count, steps):
    return [(i, (i + steps) % count) for i in range(count)]


def split2(value):
    high = lax.reduce_precision(value, 8, 7)
    return high.astype(BF), (value - high).astype(BF)


def dft_tables(frame_len, groups):
    half = frame_len // 2
    per = half // groups
    unit = 2.0 * math.pi / frame_len
    scale = 1.0 / math.sqrt(half)
    n_a = lax.broadcasted_iota(jnp.int32, (groups, half), 1)
    f_a = lax.broadcasted_iota(jnp.int32, (groups, half), 0)
    ang_a = ((f_a * per * n_a) % frame_len).astype(F32) * unit
    n_b = lax.broadcasted_iota(jnp.int32, (per, half), 1)
    j_b = lax.broadcasted_iota(jnp.int32, (per, half), 0)
    ang_b = ((j_b * n_b) % frame_len).astype(F32) * unit
    ca, sa = lax.optimization_barrier((jnp.cos(ang_a), jnp.sin(ang_a)))
    cb, sb = lax.optimization_barrier((jnp.cos(ang_b) * scale, jnp.sin(ang_b) * scale))
    rows = []
    for par in range(2):
        for kind in range(2):
            c2, s2 = cb[par::2][None], sb[par::2][None]
            c1, s1 = ca[:, None], sa[:, None]
            table = c1 * c2 - s1 * s2 if kind == 0 else -(s1 * c2 + c1 * s2)
            rows.append(table.reshape(groups * (per // 2), half))
    return split2(jnp.stack(rows).reshape(2, half, half))


def filter_kernel(side, coef, *refs, views):
    kept, sent = refs[-2:]
    step = 16
    pair = 2 * SLOTS

    def load(view, a, rows):
        ref, lead, offset = refs[view[0]], view[1], view[2]
        rows = pl.ds(rows + offset, step)
        value = ref[a, rows, :] if lead is None else ref[lead, a, rows, :]
        return value.astype(F32)

    def run(first, second, mine):
        def body(idx, carry):
            start = pl.multiple_of(idx * step, step)
            rows = pl.ds(start, step)
            cols = coef[rows, :]
            taps = [jnp.broadcast_to(cols[:, t : t + 1], (step, LANES)) for t in range(12)]
            acc = [None] * pair
            for block in range(3):
                for half in range(2):
                    view = (first, second)[half][block]
                    for a in range(SLOTS):
                        at = pair * block + SLOTS * half + a
                        frame = load(view, a, start)
                        for j in range(pair):
                            t = at - j + SHIFT - 5
                            if 0 <= t < 12:
                                term = taps[t] * frame
                                acc[j] = term if acc[j] is None else acc[j] + term
            for r in range(SLOTS):
                kept[r, rows, :] = acc[SLOTS * mine + r]
                sent[r, rows, :] = acc[SLOTS * (1 - mine) + r]
            return carry

        lax.fori_loop(0, kept.shape[1] // step, body, 0, unroll=2)

    own, rec = views[:3], views[3:]

    @pl.when(side[0] == 0)
    def _():
        run(own, rec, 0)

    @pl.when(side[0] != 0)
    def _():
        run(rec, own, 1)


def filtered(side, arrays, views, coef):
    shape = jax.ShapeDtypeStruct((SLOTS, coef.shape[0], LANES), F32)
    in_vmem = pl.BlockSpec(memory_space=pltpu.VMEM)
    return pl.pallas_call(
        functools.partial(filter_kernel, views=views),
        out_shape=(shape, shape),
        in_specs=[pl.BlockSpec(memory_space=pltpu.SMEM)] + [in_vmem] * (1 + len(arrays)),
        out_specs=(in_vmem, in_vmem),
        compiler_params=pltpu.CompilerParams(vmem_limit_bytes=4 << 20),
        cost_estimate=pl.CostEstimate(flops=FILTER_HINT, transcendentals=0, bytes_accessed=0),
        name="filter",
    )(side, coef, *arrays)


def dft_kernel(side, *refs):
    subs = (len(refs) - 5) // 2
    owns, recs = refs[:subs], refs[subs : 2 * subs]
    wh, wl, out, fold, even = refs[2 * subs :]
    tile = 16
    width = SLOTS * LANES
    groups, per, _ = out.shape
    sign = jnp.where(side[0] == 0, 1.0, -1.0)
    step = pl.program_id(0)

    @pl.when(step == 0)
    def _():
        first = 0
        for sub in range(subs):
            size = owns[sub].shape[1]

            def body(idx, carry):
                start = pl.multiple_of(idx * tile, tile)
                rows = pl.ds(start, tile)
                at = pl.ds(start + first, tile)
                for r in range(SLOTS):
                    one, two = owns[sub][r, rows, :], recs[sub][r, rows, :]
                    for par in range(2):
                        value = one + two if par == 0 else (one - two) * sign
                        top = value.astype(BF)
                        rest = (value - top.astype(F32)).astype(BF)
                        fold[par, at, r * LANES : (r + 1) * LANES] = top
                        fold[par, at, width + r * LANES : width + (r + 1) * LANES] = rest
                return carry

            lax.fori_loop(0, size // tile, body, 0, unroll=2)
            first += size

    data = fold.at[step // 2]
    full = jnp.dot(wh[0], data[...], preferred_element_type=F32)
    rest = jnp.dot(wl[0], data[:, :width], preferred_element_type=F32)
    total = (full[:, :width] + full[:, width:] + rest).reshape(groups, per // 2, width)

    @pl.when(step < 2)
    def _():
        even[step] = total

    for kind in range(2):

        @pl.when(step == 2 + kind)
        def _():
            both = jnp.concatenate([even[kind], total], axis=1).astype(BF)
            out[:, :, kind * width : (kind + 1) * width] = both


def dft(side, owns, recs, table_h, table_l, groups, room):
    half = table_h.shape[1]
    per = half // groups
    width = SLOTS * LANES
    table = pl.BlockSpec((1, half // 2, half), lambda i: (i // 2, i % 2, 0))
    return pl.pallas_call(
        dft_kernel,
        out_shape=jax.ShapeDtypeStruct((groups, per, 2 * width), BF),
        grid=(4,),
        in_specs=[pl.BlockSpec(memory_space=pltpu.SMEM)]
        + [pl.BlockSpec(value.shape, lambda i: (0, 0, 0)) for value in owns + recs]
        + [table, table],
        out_specs=pl.BlockSpec((groups, per, 2 * width), lambda i: (0, 0, 0)),
        scratch_shapes=[
            pltpu.VMEM((2, half, 2 * width), BF),
            pltpu.VMEM((2, groups, per // 2, width), F32),
        ],
        compiler_params=pltpu.CompilerParams(vmem_limit_bytes=room << 20),
        cost_estimate=pl.CostEstimate(flops=DFT_HINT, transcendentals=0, bytes_accessed=0),
        name="dft",
    )(side, *owns, *recs, table_h, table_l)


NT = (((1,), (1,)), ((), ()))


def gram_kernel(place, turned, begin, order, *refs):
    before = refs[0] if len(refs) == 3 else None
    x_out, packed = refs[-2:]
    groups, per, _ = turned.shape
    spectra = x_out.shape[1]
    block = begin.shape[0]
    tile = order.shape[0] // per
    for base in range(0, groups, tile):
        rows = turned[base : base + tile].reshape(tile * per, -1)
        rows = jnp.dot(order[...], rows, preferred_element_type=F32).astype(BF)
        for c in range(per):
            for part in range(2):
                for r in range(SLOTS):
                    lane = (part * SLOTS + r) * LANES
                    at = r * groups + base
                    x_out[c, at : at + tile, part * LANES : (part + 1) * LANES] = rows[
                        c * tile : (c + 1) * tile, lane : lane + LANES
                    ]
    cut = min(spectra, LANES)
    tail = spectra - cut
    quarter = per // 4
    dot = lambda a, b: lax.dot_general(a, b, NT, preferred_element_type=F32)
    for c in range(per):
        top = (c // (2 * quarter) + place[0]) % 2
        low = ((c // quarter) % 2 + place[1]) % 2
        pos = top * (2 * quarter) + low * quarter + c % quarter

        def put(r0, r1, l0, l1, value):
            if before is not None:
                value = value + before[pos, r0:r1, l0:l1]
            packed[pos, r0:r1, l0:l1] = value

        x = x_out[c]
        put(0, spectra, 0, cut, dot(x, x[:cut]))
        first = dot(begin[...], x)
        at = spectra + tail // 2
        put(at, at + block, 0, cut, first[:, :cut])
        if tail:
            corner = dot(x[cut:], x[cut:])
            put(spectra, at, 0, tail, corner[: tail // 2])
            put(spectra, at, tail, 2 * tail, corner[tail // 2 :])
            put(at + block, at + 2 * block, 0, tail, first[:, cut:])


def packed_rows(spectra, block):
    return spectra + max(spectra - LANES, 0) // 2 + 2 * block


def gram(place, turned, begin, before):
    groups, per, _ = turned.shape
    spectra = groups * SLOTS
    block = begin.shape[0]
    tile = min(16, groups)
    order = np.zeros((per, tile, tile, per), np.float32)
    for c in range(per):
        for src in range(tile):
            order[c, src, src, (c % 2) * (per // 2) + c // 2] = 1.0
    order = jnp.asarray(order.reshape(per * tile, per * tile), BF)
    in_vmem = pl.BlockSpec(memory_space=pltpu.VMEM)
    operands = [turned, begin, order] + ([] if before is None else [before])
    return pl.pallas_call(
        gram_kernel,
        out_shape=(
            jax.ShapeDtypeStruct((per, spectra, 2 * LANES), BF),
            jax.ShapeDtypeStruct((per, packed_rows(spectra, block), LANES), F32),
        ),
        in_specs=[pl.BlockSpec(memory_space=pltpu.SMEM)] + [in_vmem] * len(operands),
        out_specs=(in_vmem, in_vmem),
        compiler_params=pltpu.CompilerParams(vmem_limit_bytes=10 << 20),
        cost_estimate=pl.CostEstimate(flops=10_000_000_000, transcendentals=0, bytes_accessed=0),
        name="gram",
    )(place, *operands)


def split3(value):
    first = value.astype(BF)
    left = value - first.astype(F32)
    second = left.astype(BF)
    third = (left - second.astype(F32)).astype(BF)
    return first, second, third


def wide_dot(a, b, dims):
    return lax.dot_general(
        a, b, (dims, ((), ())), precision=lax.Precision.HIGHEST, preferred_element_type=F32
    )


def unpack(packed, spectra, block):
    cut = min(spectra, LANES)
    tail = spectra - cut
    square = packed[:spectra, :cut]
    if not tail:
        return square, packed[spectra : spectra + block, :cut]
    at = spectra + tail // 2
    corner = packed[spectra:at, : 2 * tail]
    corner = jnp.concatenate([corner[:, :tail], corner[:, tail:]], axis=0)
    side = jnp.concatenate([square[cut:].T, corner], axis=0)
    first = jnp.concatenate(
        [packed[at : at + block, :cut], packed[at + block : at + 2 * block, :tail]], axis=1
    )
    return jnp.concatenate([square, side], axis=1), first


def iterate_kernel(gram_ref, out, *, spectra):
    count = gram_ref.shape[0]
    block = out.shape[1] // 2
    inverse = 1.0 / spectra
    rows = lax.broadcasted_iota(jnp.int32, (block, 1), 0)
    both = [unpack(gram_ref[c], spectra, block) for c in range(count)]
    covs = [split3(pair[0]) for pair in both]

    def times(value, parts):
        a, b, c = split3(value)
        lead = jnp.dot(jnp.concatenate([a, b, c], axis=0), parts[0], preferred_element_type=F32)
        next_ = jnp.dot(jnp.concatenate([a, b], axis=0), parts[1], preferred_element_type=F32)
        last = jnp.dot(a, parts[2], preferred_element_type=F32)
        small = lead[2 * block :] + next_[block:] + last
        return lead[:block] + (lead[block : 2 * block] + next_[:block] + small)

    proj = [pair[1] for pair in both]
    coef = [None] * count
    for iteration in range(ITERS):
        mapped = [times(proj[c], covs[c]) * inverse for c in range(count)]
        gram = [wide_dot(mapped[c], proj[c], ((1,), (1,))) * inverse for c in range(count)]
        before = [proj[c] * inverse for c in range(count)]
        scale = [jnp.zeros((block, 1), F32)] * count
        for j in range(block):
            for c in range(count):
                pivot = gram[c][j : j + 1, j : j + 1]
                factor = jnp.where(rows > j, gram[c][:, j : j + 1] / pivot, 0.0)
                scale[c] = jnp.where(rows == j, 1.0 / jnp.sqrt(pivot), scale[c])
                gram[c] = gram[c] - factor * gram[c][j : j + 1, :]
                mapped[c] = mapped[c] - factor * mapped[c][j : j + 1, :]
                if iteration == ITERS - 1:
                    before[c] = before[c] - factor * before[c][j : j + 1, :]
        proj = [mapped[c] * scale[c] for c in range(count)]
        coef = [before[c] * scale[c] for c in range(count)]
    for c in range(count):
        out[c, :block, :] = coef[c]
        out[c, block:, :] = times(coef[c], covs[c])


def iterate(gram, spectra, block):
    count = gram.shape[0]
    return pl.pallas_call(
        lambda g, o: iterate_kernel(g, o, spectra=spectra),
        out_shape=jax.ShapeDtypeStruct((count, 2 * block, spectra), F32),
        compiler_params=pltpu.CompilerParams(vmem_limit_bytes=12 << 20),
        name="iterate",
    )(gram)


def clean_kernel(xa, xb, pair, perm, out, ritz):
    count, spectra, _ = xa.shape
    block = pair.shape[1] // 2
    order = perm[...]
    for c in range(count):
        coef = pair[c, :block, :]
        proj = pair[c, block:, :]
        ritz[c] = wide_dot(proj, proj, NT[0]) * (1.0 / spectra)
        coef3 = jnp.concatenate(split3(coef), axis=0)
        proj3 = jnp.concatenate(split3(proj), axis=0)
        turned = lax.dot_general(order, proj3, NT, preferred_element_type=F32)
        ph, pm, pt = [(-turned[:, i * block : (i + 1) * block]).astype(BF) for i in range(3)]
        left = jnp.concatenate([order, ph, ph, ph, pm, pm, pt], axis=1)
        for chunk, ref in enumerate((xa, xb)):
            x = ref[c]
            base = jnp.dot(coef3, x, preferred_element_type=F32)
            base = base[:block] + base[block : 2 * block] + base[2 * block :]
            bh, bm, bt = split3(base)
            right = jnp.concatenate([x, bh, bm, bt, bh, bm, bh], axis=0)
            result = jnp.dot(left, right, preferred_element_type=F32).astype(BF)
            for part in range(2):
                lane = part * 2 * LANES + chunk * LANES
                out[c, :, lane : lane + LANES] = result[:, part * LANES : (part + 1) * LANES]


def clean(xs, pair, spectra):
    channels = pair.shape[0]
    block = pair.shape[1] // 2
    width = 2 * LANES
    step = 4
    order = np.zeros((spectra, spectra), np.float32)
    groups = spectra // SLOTS
    for src in range(groups):
        for r in range(SLOTS):
            order[(SLOTS * src + r + SHIFT) % spectra, r * groups + src] = 1.0
    x_spec = pl.BlockSpec((step, spectra, width), lambda c: (c, 0, 0))
    return pl.pallas_call(
        clean_kernel,
        out_shape=(
            jax.ShapeDtypeStruct((channels, spectra, 2 * width), BF),
            jax.ShapeDtypeStruct((channels, block, block), F32),
        ),
        grid=(channels // step,),
        in_specs=[
            x_spec,
            x_spec,
            pl.BlockSpec((step, 2 * block, spectra), lambda c: (c, 0, 0)),
            pl.BlockSpec((spectra, spectra), lambda c: (0, 0)),
        ],
        out_specs=(
            pl.BlockSpec((step, spectra, 2 * width), lambda c: (c, 0, 0)),
            pl.BlockSpec((step, block, block), lambda c: (c, 0, 0)),
        ),
        compiler_params=pltpu.CompilerParams(vmem_limit_bytes=12 << 20),
        name="clean",
    )(*xs, pair, jnp.asarray(order, BF))


def reduce_inputs(packed):
    for axis in ("k", "l"):
        half = packed.shape[0] // 2
        packed = packed[:half] + lax.ppermute(packed[half:], axis, cyclic(2, 1))
    return packed


def gather_inputs(value):
    for axis in ("l", "k"):
        value = lax.all_gather(value, axis, tiled=True)
    return value


def shards(voltages, taps, start):
    slots, frame_len, inputs = voltages.shape
    half = frame_len // 2
    block = start.shape[0]
    groups = lax.axis_size("y") * lax.axis_size("z") * 2
    rings = groups // 2
    spectra = groups * slots
    per = half // groups
    chunks = inputs // LANES
    me = lax.axis_index("h")
    side = me.reshape(1)
    k_index, l_index = lax.axis_index("k"), lax.axis_index("l")
    coef = lax.dynamic_slice_in_dim(taps.T, me * half, half, 0)
    table_h, table_l = dft_tables(frame_len, groups)

    def piece(chunk, which, first, size):
        at = (0, which * half + first, chunk * LANES)
        return lax.dynamic_slice(voltages, at, (slots, size, LANES)).astype(BF)

    def swap(value):
        return lax.ppermute(value, "h", cyclic(2, 1))

    def both_ways(value):
        return (
            lax.ppermute(value, ("y", "z"), cyclic(rings, 1)),
            lax.ppermute(value, ("y", "z"), cyclic(rings, -1)),
        )

    rank = l_index * 2 + k_index
    begin = lax.dynamic_slice_in_dim(start, rank * inputs, inputs, 2).astype(BF)
    begin = begin.reshape(block, 2, chunks, LANES).transpose(2, 0, 1, 3).reshape(chunks, block, -1)

    fence = lax.optimization_barrier
    sub = half // 2
    cut = half * 8 // 16
    coefs = [coef[:sub], coef[sub:]]
    coefs_b = [coef[:cut], coef[cut:]]
    parts_b = ((0, cut), (cut, half - cut))

    own_a = piece(0, me, 0, half)
    send_a = [piece(0, 1 - me, i * sub, sub) for i in range(2)]
    up_own, down_own = both_ways(own_a)
    rec_a = [swap(send_a[0])]
    rec_a.append(swap(fence((send_a[1], rec_a[0]))[0]))
    ways_a = [both_ways(value) for value in rec_a]
    own_b = [piece(1, me, *part) for part in parts_b]
    rec_b = []
    for i in range(2):
        rec_b.append(swap(fence((piece(1, 1 - me, *parts_b[i]), rec_a[1]))[0]))
    both_b = [jnp.stack([own_b[i], rec_b[i]]) for i in range(2)]
    ways_b = [both_ways(fence((both_b[i], ways_a[i]))[0]) for i in range(2)]

    kept, back = [[], []], [[], []]
    for i in range(2):
        arrays = (up_own, own_a, down_own, ways_a[i][0], rec_a[i], ways_a[i][1])
        views = tuple((n, None, i * sub if n < 3 else 0) for n in range(6))
        if i == 0:
            arrays, (table_h, table_l) = fence((arrays, (table_h, table_l)))
        mine, sent = filtered(side, arrays, views, coefs[i])
        kept[0].append(mine)
        back[0].append(swap(sent))
    specs = []
    back_first = back[0][0]
    for i in range(2):
        arrays = (ways_b[i][0], both_b[i], ways_b[i][1])
        views = tuple((n % 3, n // 3, 0) for n in range(6))
        if i == 1:
            specs.append(dft(side, kept[0], back[0], table_h, table_l, groups, 30))
            arrays = fence((arrays, back_first))[0]
        mine, sent = filtered(side, arrays, views, coefs_b[i])
        kept[1].append(mine)
        if i == 0:
            kept[0], back[0], sent = fence((kept[0], back[0], sent))
        back[1].append(swap(sent))
    specs.append(dft(side, kept[1], back[1], table_h, table_l, groups, 58))
    turned = [lax.all_to_all(spec, FREQ, split_axis=0, concat_axis=0, tiled=True) for spec in specs]
    place = jnp.stack([k_index, l_index])
    xs, packed = [], None
    for chunk in range(chunks):
        x, packed = gram(place, turned[chunk], begin[chunk], packed)
        xs.append(x)
    pair = gather_inputs(iterate(reduce_inputs(packed), spectra, block))
    cleaned, ritz = clean(xs, pair, spectra)
    return cleaned.reshape(per, spectra, 2, inputs), ritz


def on_mesh(mesh):
    return jax.shard_map(
        shards,
        mesh=mesh,
        in_specs=(P(FREQ, None, INP), P(), P()),
        out_specs=(P(FREQ, None, None, INP), P(FREQ, None, None)),
        check_vma=False,
    )


def solution(mesh):
    freq = mesh.shape["freq"]
    devices = mesh.devices.reshape(freq // 16, 8, 2, 2, 2)
    return on_mesh(Mesh(devices, FREQ + INP))
```
